256 devices in a mesh: gx: 16 (over z, x_hi), gy: 16 (over y, x_lo, core).
Axes of the slice: x: 4 (x_hi: 2, x_lo: 2; x = x_hi * 2 + x_lo), y: 4, z: 8, core: 2. Of those that a mesh axis runs over, the one named last changes fastest.
Arguments:
- features: bfloat16 [1024, 8, 8, 8, 128], P(('gx', 'gy')), may hold values from -6 to 6
- out_grad: bfloat16 [1024, 8, 8, 8, 128], P(('gx', 'gy')), may hold values from -6 to 6
- kernel: bfloat16 [27, 128, 128], replicated, may hold values from -0.109375 to 0.109375
- voxel_mask: int32 [1024, 512], P(('gx', 'gy')), may hold values from 0 to 1, as said below
- neighbours: int32 [1024, 27], P(('gx', 'gy')), may hold values from 0 to 16, as said below
- face_sends: int32 [1024, 2], P(('gx', 'gy')), may hold values from 0 to 4, as said below
- edge_sends: int32 [1024, 1], P(('gx', 'gy')), may hold values from 0 to 4, as said below
Outputs:
- output: bfloat16 [1024, 8, 8, 8, 128], P(('gx', 'gy'))
- input_grad: bfloat16 [1024, 8, 8, 8, 128], P(('gx', 'gy'))
- weight_grad: float32 [27, 128, 128], replicated
The draws below stay inside these ranges and needn't reach their ends.
Inputs may be any that keep to these rules, and one draw needn't show every extreme that they name: `voxel_mask`: zero in every voxel of a slot that holds no brick; in a slot that holds a brick each voxel is one or zero. neighbours[s, 9 (n_x + 1) + 3 (n_y + 1) + n_z + 1] is the index in the device's pool of the brick at brick offset n from slot s's brick, or 16 where that position lies outside the volume or holds no brick; the entry for offset (0,0,0) is the slot's own number; all other entries of a slot that holds no brick are 16. Each column of brick positions holds at most 1 bricks. `face_sends`: row 4 t + j lists, in increasing order, the device's slots whose bricks lie in its brick columns next to the side (-1,0), (1,0), (0,-1), (0,1) numbered j, then 4 for the rest. `edge_sends`: row 4 t + j lists, in increasing order, the device's slots whose bricks lie in its brick column at the corner (-1,-1), (-1,1), (1,-1), (1,1) numbered j, then 4 for the rest.
All inputs are finite; a program needn't handle non-finite values.
Results may differ from the reference program's by a relative error of at most 0.001.
Values may be sent and summed in bfloat16 or wider, within the bound.
A program may use at most 192 MiB of HBM per device.

```python
import math
import jax
import jax.numpy as jnp
import numpy as np
from jax import lax

CHANNELS = 128
COLUMN_CAP = 1
DEPTH = 8
BRICKS = 4
FACE_CAP = 2
EDGE_CAP = 1
POOL = 17
SLOTS = 1024
VOXELS = 524288
N_GX = 16
N_GY = 16


DIRECTIONS = ((-1, 0), (1, 0), (0, -1), (0, 1), (-1, -1), (-1, 1), (1, -1), (1, 1))


def brick_layout(key):
    column_cap = COLUMN_CAP
    bricks_dev = 4 * column_cap
    face_cap = 2 * column_cap
    edge_cap = column_cap
    grid_x = N_GX
    grid_y = N_GY
    depth = DEPTH
    places = 4 * depth
    zero_entry = bricks_dev + 4 * face_cap + 4 * edge_cap
    base_key = jax.random.fold_in(key, 7)
    key_count, key_full, key_place, key_order, key_voxel = jax.random.split(base_key, 5)
    counts = jax.random.randint(key_count, (grid_x, grid_y, 4), 0, column_cap + 1)
    chosen = jax.random.randint(key_full, (), 0, grid_x * grid_y)
    device_ids = jnp.arange(grid_x * grid_y).reshape(grid_x, grid_y)
    counts = jnp.where((device_ids == chosen)[:, :, None], column_cap, counts)
    scores = jax.random.randint(key_place, (grid_x, grid_y, 4, depth), 0, 1 << 20) * depth + jnp.arange(depth)
    ranks = jnp.argsort(jnp.argsort(scores, axis=-1), axis=-1)
    occupied = (ranks < counts[..., None]).reshape(grid_x, grid_y, places)
    order_scores = jax.random.randint(key_order, (grid_x, grid_y, places), 0, 1 << 20) * places + jnp.arange(places)
    order_scores = jnp.where(occupied, order_scores, (1 << 20) * places + jnp.arange(places))
    ordering = jnp.argsort(order_scores, axis=-1)
    slot_of_place = jnp.argsort(ordering, axis=-1)
    place_of_slot = ordering[..., :bricks_dev]
    slot_live = jnp.take_along_axis(occupied, place_of_slot, axis=-1)
    column = place_of_slot // depth
    column_x = column // 2
    column_y = column % 2
    level = place_of_slot % depth
    voxels = jax.random.randint(key_voxel, (grid_x, grid_y, bricks_dev, 512), 0, 2) * slot_live[..., None].astype(jnp.int32)
    toward_x = jnp.array([d[0] for d in DIRECTIONS], jnp.int32)[:, None]
    toward_y = jnp.array([d[1] for d in DIRECTIONS], jnp.int32)[:, None]
    match_x = (toward_x == 0) | (column_x[:, :, None, :] == (toward_x > 0).astype(jnp.int32))
    match_y = (toward_y == 0) | (column_y[:, :, None, :] == (toward_y > 0).astype(jnp.int32))
    matches = slot_live[:, :, None, :] & match_x & match_y
    slot_index = jnp.arange(bricks_dev)
    list_keys = jnp.where(matches, slot_index, bricks_dev + slot_index)
    listed = jnp.sort(list_keys, axis=-1)
    listed = jnp.where(listed < bricks_dev, listed, bricks_dev)
    face_lists = listed[:, :, :4, :face_cap].reshape(-1, face_cap)
    edge_lists = listed[:, :, 4:, :edge_cap].reshape(-1, edge_cap)
    list_rank = jnp.cumsum(matches.astype(jnp.int32), axis=-1) - 1
    offset_table = np.array([(i, j, k) for i in (-1, 0, 1) for j in (-1, 0, 1) for k in (-1, 0, 1)], np.int32)
    offset_x = jnp.asarray(offset_table[:, 0])
    offset_y = jnp.asarray(offset_table[:, 1])
    offset_z = jnp.asarray(offset_table[:, 2])
    grid_a = jnp.arange(grid_x)[:, None, None, None]
    grid_b = jnp.arange(grid_y)[None, :, None, None]
    whole_x = 2 * grid_a + column_x[..., None] + offset_x
    whole_y = 2 * grid_b + column_y[..., None] + offset_y
    whole_z = level[..., None] + offset_z
    inside = (whole_x >= 0) & (whole_x < 2 * grid_x) & (whole_y >= 0) & (whole_y < 2 * grid_y) & (whole_z >= 0) & (whole_z < depth)
    clamp_x = jnp.clip(whole_x, 0, 2 * grid_x - 1)
    clamp_y = jnp.clip(whole_y, 0, 2 * grid_y - 1)
    clamp_z = jnp.clip(whole_z, 0, depth - 1)
    source_a = clamp_x // 2
    source_b = clamp_y // 2
    source_place = (clamp_x % 2 * 2 + clamp_y % 2) * depth + clamp_z
    present = occupied[source_a, source_b, source_place]
    source_slot = slot_of_place[source_a, source_b, source_place]
    step_a = source_a - grid_a
    step_b = source_b - grid_b
    base_table = np.zeros((3, 3), np.int32)
    direction_table = np.zeros((3, 3), np.int32)
    faces_list = DIRECTIONS[:4]
    edges_list = DIRECTIONS[4:]
    for position in range(4):
        source = faces_list[position]
        base_table[source[0] + 1, source[1] + 1] = bricks_dev + position * face_cap
        direction_table[source[0] + 1, source[1] + 1] = DIRECTIONS.index((-source[0], -source[1]))
        source = edges_list[position]
        base_table[source[0] + 1, source[1] + 1] = bricks_dev + 4 * face_cap + position * edge_cap
        direction_table[source[0] + 1, source[1] + 1] = DIRECTIONS.index((-source[0], -source[1]))
    block_base = jnp.asarray(base_table)[step_a + 1, step_b + 1]
    block_direction = jnp.asarray(direction_table)[step_a + 1, step_b + 1]
    rank_there = list_rank[source_a, source_b, block_direction, source_slot]
    entries = jnp.where((step_a == 0) & (step_b == 0), source_slot, block_base + rank_there)
    entries = jnp.where(inside & present & slot_live[..., None], entries, zero_entry)
    center = (offset_x == 0) & (offset_y == 0) & (offset_z == 0)
    entries = jnp.where(center, jnp.broadcast_to(slot_index[:, None], entries.shape), entries)
    return (voxels.reshape(-1, 512).astype(jnp.int32), entries.reshape(-1, 27).astype(jnp.int32), face_lists.astype(jnp.int32), edge_lists.astype(jnp.int32))


def draw_voxel_mask(key, part):
    return brick_layout(key)[0]


def draw_neighbours(key, part):
    return brick_layout(key)[1]


def draw_face_sends(key, part):
    return brick_layout(key)[2]


def draw_edge_sends(key, part):
    return brick_layout(key)[3]


def steps_of(own_key, shape, cuts, low, high):
    factor_of = 1.0
    for dim, blocks in cuts:
        steps = jax.random.uniform(jax.random.fold_in(jax.random.fold_in(own_key, 6), dim), (blocks,), jnp.float32, low / len(cuts), high / len(cuts))
        factor_of = factor_of * jnp.repeat(jnp.exp(steps), shape[dim] // blocks).reshape((-1,) + (1,) * (len(shape) - 1 - dim))
    return factor_of


def noise(key, shape, width, limit, cuts=(), held_as=jnp.bfloat16):
    values = width * jax.random.normal(key, shape, jnp.float32)
    if cuts:
        values = values * steps_of(key, shape, cuts, -0.22, 0.18)
    return jnp.clip(values, -limit, limit).astype(held_as)


def setup_inputs(seed: int = 0) -> dict:
    key_list = jax.random.split(jax.random.key(seed), 8)
    features = noise(key_list[0], (SLOTS, 8, 8, 8, CHANNELS), 1.0, 6.0, ((0, 256),))
    out_grad = noise(key_list[1], (SLOTS, 8, 8, 8, CHANNELS), 1.0, 6.0, ((0, 256),))
    kernel = noise(key_list[2], (27, CHANNELS, CHANNELS), (27 * CHANNELS) ** -0.5, 0.109375)
    voxel_mask = draw_voxel_mask(jax.random.fold_in(key_list[7], 71), 0)
    neighbours = draw_neighbours(jax.random.fold_in(key_list[7], 71), 0)
    face_sends = draw_face_sends(jax.random.fold_in(key_list[7], 71), 0)
    edge_sends = draw_edge_sends(jax.random.fold_in(key_list[7], 71), 0)
    return {"features": features, "out_grad": out_grad, "kernel": kernel, "voxel_mask": voxel_mask, "neighbours": neighbours, "face_sends": face_sends, "edge_sends": edge_sends}


def cell_range(step):
    if step < 0:
        return slice(7, 8)
    if step > 0:
        return slice(0, 1)
    return slice(0, 8)

def padded_bricks(extended, indices):
    layers_x = []
    for step_x in (-1, 0, 1):
        layers_y = []
        for step_y in (-1, 0, 1):
            layers_z = []
            for step_z in (-1, 0, 1):
                column = 9 * (step_x + 1) + 3 * (step_y + 1) + step_z + 1
                picked = jnp.take(extended, indices[:, column], axis=0)
                layers_z.append(picked[:, cell_range(step_x), cell_range(step_y), cell_range(step_z)])
            layers_y.append(jnp.concatenate(layers_z, axis=3))
        layers_x.append(jnp.concatenate(layers_y, axis=2))
    return jnp.concatenate(layers_x, axis=1)

def shifted_columns(padded, step_x, direction):
    row_count = padded.shape[0] * 512
    channels = padded.shape[-1]
    pieces = []
    low_x = 1 + direction * step_x
    for step_y in (-1, 0, 1):
        for step_z in (-1, 0, 1):
            low_y = 1 + direction * step_y
            low_z = 1 + direction * step_z
            pieces.append(padded[:, low_x:low_x + 8, low_y:low_y + 8, low_z:low_z + 8].reshape(row_count, channels))
    return jnp.concatenate(pieces, axis=1)

def global_slots(neighbours, face_sends, edge_sends):
    slot_ids = jnp.arange(SLOTS, dtype=jnp.int32)
    device = slot_ids // BRICKS
    grid_a = (device // N_GY)[:, None]
    grid_b = (device % N_GY)[:, None]

    def remote_slot(offset, capacity, steps_a, steps_b, reverse_index, lists):
        position = jnp.clip(offset, 0, 4 * capacity - 1)
        block_index = position // capacity
        place_index = position % capacity
        source_a = grid_a + steps_a[block_index]
        source_b = grid_b + steps_b[block_index]
        inside = (source_a >= 0) & (source_a < N_GX) & (source_b >= 0) & (source_b < N_GY)
        source = jnp.clip(source_a, 0, N_GX - 1) * N_GY + jnp.clip(source_b, 0, N_GY - 1)
        listed = lists[source * 4 + reverse_index[block_index], place_index]
        return jnp.where(inside & (listed < BRICKS), source * BRICKS + listed, SLOTS)
    face_part = remote_slot(neighbours - BRICKS, FACE_CAP, jnp.array([-1, 1, 0, 0], jnp.int32), jnp.array([0, 0, -1, 1], jnp.int32), jnp.array([1, 0, 3, 2], jnp.int32), face_sends)
    edge_part = remote_slot(neighbours - BRICKS - 4 * FACE_CAP, EDGE_CAP, jnp.array([-1, -1, 1, 1], jnp.int32), jnp.array([-1, 1, -1, 1], jnp.int32), jnp.array([3, 2, 1, 0], jnp.int32), edge_sends)
    local_slot = device[:, None] * BRICKS + neighbours
    result = jnp.where(neighbours < BRICKS, local_slot, jnp.where(neighbours < BRICKS + 4 * FACE_CAP, face_part, jnp.where(neighbours < POOL - 1, edge_part, SLOTS)))
    return result.astype(jnp.int32)

def reference(features, out_grad, kernel, voxel_mask, neighbours, face_sends, edge_sends):
    channels = CHANNELS
    devices = N_GX * N_GY
    mask_brick = voxel_mask.astype(jnp.bfloat16).reshape(SLOTS, 8, 8, 8, 1)
    active = features * mask_brick
    masked_grad = out_grad * mask_brick
    zero_brick = jnp.zeros((1, 8, 8, 8, channels), jnp.bfloat16)
    active_ext = jnp.concatenate([active, zero_brick], axis=0)
    grad_ext = jnp.concatenate([masked_grad, zero_brick], axis=0)
    table = global_slots(neighbours, face_sends, edge_sends)
    forward_rows = kernel.reshape(3, 9 * channels, channels)
    backward_rows = jnp.transpose(kernel.reshape(3, 9, channels, channels), (0, 1, 3, 2)).reshape(3, 9 * channels, channels)
    row_count = BRICKS * 512

    def per_device(kernel_sum, device):
        indices = lax.dynamic_slice_in_dim(table, device * BRICKS, BRICKS, 0)
        mask_rows = lax.dynamic_slice_in_dim(voxel_mask, device * BRICKS, BRICKS, 0).reshape(row_count, 1).astype(jnp.float32)
        grad_rows = lax.dynamic_slice_in_dim(masked_grad, device * BRICKS, BRICKS, 0).reshape(row_count, channels)
        padded = padded_bricks(active_ext, indices)
        padded_grad = padded_bricks(grad_ext, indices)
        running_sum = jnp.zeros((row_count, channels), jnp.float32)
        back_sum = jnp.zeros((row_count, channels), jnp.float32)
        kernel_parts = []
        for step_x in (-1, 0, 1):
            columns = shifted_columns(padded, step_x, 1)
            running_sum = running_sum + jnp.dot(columns, forward_rows[step_x + 1], preferred_element_type=jnp.float32)
            kernel_parts.append(lax.dot_general(columns, grad_rows, (((0,), (0,)), ((), ())), preferred_element_type=jnp.float32))
            back_columns = shifted_columns(padded_grad, step_x, -1)
            back_sum = back_sum + jnp.dot(back_columns, backward_rows[step_x + 1], preferred_element_type=jnp.float32)
        out_rows = (running_sum * mask_rows).astype(jnp.bfloat16).reshape(BRICKS, 8, 8, 8, channels)
        grad_out = (back_sum * mask_rows).astype(jnp.bfloat16).reshape(BRICKS, 8, 8, 8, channels)
        kernel_sum = kernel_sum + jnp.stack(kernel_parts).reshape(27, channels, channels)
        return (kernel_sum, (out_rows, grad_out))
    start_sum = jnp.zeros((27, channels, channels), jnp.float32)
    weight_sum, stacked = lax.scan(per_device, start_sum, jnp.arange(devices, dtype=jnp.int32))
    output = stacked[0].reshape(SLOTS, 8, 8, 8, channels)
    input_grad = stacked[1].reshape(SLOTS, 8, 8, 8, channels)
    return (output, input_grad, weight_sum / math.sqrt(VOXELS))
```

```python
import math

import jax
import jax.numpy as jnp
from jax import lax
from jax.experimental import pallas as pl
from jax.experimental.pallas import tpu as pltpu
from jax.sharding import PartitionSpec as P

MESH = pl.DeviceIdType.MESH
FACES = ((-1, 0), (1, 0), (0, -1), (0, 1))
EDGES = ((-1, -1), (-1, 1), (1, -1), (1, 1))
TOWARD = FACES + EDGES
CH = 128
BRICKS = 4
OWN = 1792
PART1 = OWN // 4
PART2 = PART1 // 4
ZROWS = 16
F32 = jnp.float32
BF16 = jnp.bfloat16


def step_kernel(
    n_gx, n_gy, scale,
    feat, ograd, kern, vmask, nbr, fsend, esend,
    out_hbm, ig_hbm, wg_hbm,
    act, maskf, xt, yt, ct, ox, oy, oc, odd, even, gt, w2, acc, outv,
    part, rc, red, r1, red1, r2, red2, rz, zsum, gz, full,
    halo_s, halo_r, c_s, c_r, a_s, a_r, b_s, b_r, z_s, z_r,
    gc_s, gc_r, ga_s, ga_r, gb_s, gb_r, gz_s, gz_r, o_sem,
):
    a = lax.axis_index("gx")
    b = lax.axis_index("gy")
    z = a // 2
    y = b // 4
    x = (a % 2) * 2 + (b // 2) % 2
    core = b % 2

    def device(x_, y_, z_, c_):
        return (z_ * 2 + x_ // 2, y_ * 4 + (x_ % 2) * 2 + c_)

    me1 = x + core * (y - x)
    me2 = y + core * (x - y)

    def peer1(p):
        return device(x + (1 - core) * (p - x), y + core * (p - y), z, core)

    def peer2(p):
        return device(x + core * (p - x), y + (1 - core) * (p - y), z, core)

    def exists(d):
        return (a + d[0] >= 0) & (a + d[0] < n_gx) & (b + d[1] >= 0) & (b + d[1] < n_gy)

    partner = device(x, y, z, 1 - core)
    peers1 = [peer1((me1 + k) % 4) for k in range(1, 4)]
    peers2 = [peer2((me2 + k) % 4) for k in range(1, 4)]
    peersz = [device(x, y, (z + k) % 8, core) for k in range(1, 8)]

    barrier = pltpu.get_barrier_semaphore()
    for peer in [partner] + peers1 + peers2 + peersz:
        pl.semaphore_signal(barrier, inc=1, device_id=peer, device_id_type=MESH)
    expected = 14
    for d in TOWARD:
        there = exists(d)
        expected = expected + there.astype(jnp.int32)

        @pl.when(there)
        def _():
            pl.semaphore_signal(barrier, inc=1, device_id=(a + d[0], b + d[1]), device_id_type=MESH)

    for s in range(BRICKS):
        for g in range(4):
            row = vmask[s : s + 1, g * 128 : (g + 1) * 128].astype(F32)
            tile = jnp.broadcast_to(row, (128, 128)).T
            maskf[s, 2 * g : 2 * g + 2] = tile.reshape(2, 8, 8, CH)

    @pl.loop(0, BRICKS)
    def _(s):
        @pl.loop(0, 8)
        def _(i):
            m = maskf[s, i]
            act[s, 0, i] = (feat[s, i].astype(F32) * m).astype(BF16)
            act[s, 1, i] = (ograd[s, i].astype(F32) * m).astype(BF16)

    act[BRICKS] = jnp.zeros((2, 8, 8, 8, CH), BF16)
    for side in range(2):
        xt[side, 16] = jnp.zeros((2, 8, 8, CH), BF16)
        yt[side, 16] = jnp.zeros((2, 8, 8, CH), BF16)
    for corner in range(4):
        ct[corner, 16] = jnp.zeros((2, 8, CH), BF16)

    def far(step):
        return 7 if step > 0 else 0

    for i, d in enumerate(TOWARD):
        if i < 2:
            for j in range(2):
                ox[i, j] = act[fsend[i, j], :, far(d[0])]
        elif i < 4:
            for j in range(2):
                oy[i - 2, j] = act[fsend[i, j], :, :, far(d[1])]
        else:
            oc[i - 4, 0] = act[esend[i - 4, 0], :, far(d[0]), far(d[1])]

    def landing(d):
        e = (-d[0], -d[1])
        k = TOWARD.index(e)
        if k < 2:
            return xt.at[k, pl.ds(4 + 2 * k, 2)]
        if k < 4:
            return yt.at[k - 2, pl.ds(4 + 2 * k, 2)]
        return ct.at[k - 4, pl.ds(12 + k - 4, 1)]

    def halo_copy(i):
        d = TOWARD[i]
        source = ox.at[i] if i < 2 else (oy.at[i - 2] if i < 4 else oc.at[i - 4])
        return pltpu.make_async_remote_copy(
            src_ref=source, dst_ref=landing(d), send_sem=halo_s.at[i], recv_sem=halo_r.at[i],
            device_id=(a + d[0], b + d[1]), device_id_type=MESH,
        )

    pl.semaphore_wait(barrier, expected)
    for i, d in enumerate(TOWARD):
        @pl.when(exists(d))
        def _():
            halo_copy(i).start()

        @pl.when(jnp.logical_not(exists((-d[0], -d[1]))))
        def _():
            spot = landing(d)
            spot[...] = jnp.zeros(spot.shape, BF16)

    for s in range(BRICKS):
        for side in range(2):
            xt[side, s] = act[s, :, 7 - 7 * side]
            yt[side, s] = act[s, :, :, 7 - 7 * side]
        for corner, e in enumerate(EDGES):
            ct[corner, s] = act[s, :, far(-e[0]), far(-e[1])]

    @pl.loop(0, 9)
    def _(n):
        for k in range(3):
            w2[0, n, k * CH : (k + 1) * CH] = kern[3 * n + k]
            w2[1, n, k * CH : (k + 1) * CH] = kern[26 - 3 * n - k].astype(F32).T.astype(BF16)

    @pl.loop(0, BRICKS)
    def _(s):
        for g in range(4):
            rows = act[s, 1, 2 * g : 2 * g + 2].astype(F32).reshape(128, CH)
            gt[s, :, g * 128 : (g + 1) * 128] = rows.T.astype(BF16)

    for i, d in enumerate(TOWARD):
        @pl.when(exists(d))
        def _():
            halo_copy(i).wait_send()

        @pl.when(exists((-d[0], -d[1])))
        def _():
            halo_copy(i).wait_recv()

    for corner, e in enumerate(EDGES):
        side_x = (e[0] + 1) // 2
        side_y = (e[1] + 1) // 2
        for j in range(2):
            ct[corner, 4 + 2 * side_x + j] = xt[side_x, 4 + 2 * side_x + j, :, far(-e[1])]
            ct[corner, 8 + 2 * side_y + j] = yt[side_y, 8 + 2 * side_y + j, :, far(-e[0])]

    level = lax.broadcasted_iota(jnp.int32, (1, 8, CH), 1)

    def shift_down(here, below):
        return jnp.where(level == 0, pltpu.roll(below, 1, 1), pltpu.roll(here, 1, 1))

    def shift_up(here, above):
        return jnp.where(level == 7, pltpu.roll(above, 7, 1), pltpu.roll(here, 7, 1))

    def put(w, s, layer, triple):
        for k in range(3):
            value = triple[k]
            odd[w, s, layer, :, k * CH : (k + 1) * CH] = value.reshape(80, CH).astype(BF16)
            even[w, s, layer, :, k * CH : (k + 1) * CH] = value[1:9].reshape(64, CH).astype(BF16)

    def shifted(three):
        return shift_down(three[1], three[0]), three[1], shift_up(three[1], three[2])

    for w in range(2):
        @pl.loop(0, BRICKS)
        def _(s):
            for side in range(2):
                column = 18 * side
                mids = [xt[side, nbr[s, column + 3 + k], w].astype(F32) for k in range(3)]
                lows = [ct[2 * side, nbr[s, column + k], w].astype(F32).reshape(1, 8, CH) for k in range(3)]
                highs = [ct[2 * side + 1, nbr[s, column + 6 + k], w].astype(F32).reshape(1, 8, CH) for k in range(3)]
                whole = [jnp.concatenate([lows[k], mids[k], highs[k]], axis=0) for k in range(3)]
                put(w, s, 9 * side, shifted(whole))

            low_at = [nbr[s, 9 + k] for k in range(3)]
            high_at = [nbr[s, 15 + k] for k in range(3)]
            below_at = nbr[s, 12]
            above_at = nbr[s, 14]

            @pl.loop(0, 8)
            def _(i):
                mid = act[s, w, i].astype(F32)
                zero = jnp.zeros((8, 8, CH), F32)
                lows = [yt[0, low_at[k], w, i].astype(F32).reshape(1, 8, CH) for k in range(3)]
                highs = [yt[1, high_at[k], w, i].astype(F32).reshape(1, 8, CH) for k in range(3)]
                parts = [zero, mid, zero]
                whole = [jnp.concatenate([lows[k], parts[k], highs[k]], axis=0) for k in range(3)]
                put(w, s, i + 1, shifted(whole))

    def columns(w, s, first, k):
        if k == 1:
            value = even[w, s, pl.ds(first, 8)]
        else:
            value = odd[w, s, pl.ds(first, 8), 8 * k : 8 * k + 64]
        return value.reshape(512, 3 * CH)

    @pl.loop(0, 3)
    def _(n):
        for k in range(3):
            total = jnp.dot(gt[0], columns(0, 0, n, k), preferred_element_type=F32)
            for s in range(1, BRICKS):
                total = total + jnp.dot(gt[s], columns(0, s, n, k), preferred_element_type=F32)
            for q in range(3):
                at = pl.multiple_of((9 * n + 3 * k + q) * CH, CH)
                part[pl.ds(at, CH)] = total[:, q * CH : (q + 1) * CH].T

    part[27 * CH : 28 * CH] = jnp.zeros((CH, CH), F32)

    def output_copy(w, s):
        target = out_hbm if w == 0 else ig_hbm
        return pltpu.make_async_copy(outv.at[w, s], target.at[s], o_sem.at[w, s])

    def convolve(s):
        @pl.loop(0, 2)
        def _(w):
            for first in range(3):
                value = jnp.concatenate([columns(w, s, first, k) for k in range(3)], axis=1)
                weight = w2[w, 3 * first : 3 * first + 3].reshape(9 * CH, CH)
                term = jnp.dot(value, weight, preferred_element_type=F32)
                if first == 0:
                    acc[...] = term
                elif first == 1:
                    acc[...] += term
                else:
                    term = (acc[...] + term) * maskf[s].reshape(512, CH)
                    outv[w, s] = term.reshape(8, 8, 8, CH).astype(BF16)
        output_copy(0, s).start()
        output_copy(1, s).start()

    def remote(source, target, sems, semr, k, peer):
        return pltpu.make_async_remote_copy(
            src_ref=source, dst_ref=target, send_sem=sems.at[k], recv_sem=semr.at[k],
            device_id=peer, device_id_type=MESH,
        )

    def run(copies, between=None):
        for copy in copies:
            copy.start()
        if between is not None:
            between()
        for copy in copies:
            copy.wait()

    def rows(start, size, unit):
        return pl.ds(pl.multiple_of(start, unit), size)

    mine = core * OWN
    run([remote(part.at[rows((1 - core) * OWN, OWN, OWN)], rc, c_s, c_r, 0, partner)])

    @pl.loop(0, OWN // 64)
    def _(i):
        at = rows(i * 64, 64, 64)
        red[at] = part[rows(mine + i * 64, 64, 64)] + rc[at]

    run(
        [remote(red.at[rows((me1 + k) % 4 * PART1, PART1, PART1)], r1.at[k - 1], a_s, a_r, k - 1, peers1[k - 1]) for k in range(1, 4)],
        lambda: convolve(0),
    )

    @pl.loop(0, PART1 // 64)
    def _(i):
        at = rows(i * 64, 64, 64)
        red1[at] = red[rows(me1 * PART1 + i * 64, 64, 64)] + r1[0, at] + r1[1, at] + r1[2, at]

    run(
        [remote(red1.at[rows((me2 + k) % 4 * PART2, PART2, PART2)], r2.at[k - 1], b_s, b_r, k - 1, peers2[k - 1]) for k in range(1, 4)],
        lambda: convolve(1),
    )
    red2[0:PART2] = red1[rows(me2 * PART2, PART2, PART2)] + r2[0] + r2[1] + r2[2]
    red2[PART2 : 8 * ZROWS] = jnp.zeros((8 * ZROWS - PART2, CH), F32)
    run(
        [remote(red2.at[rows((z + k) % 8 * ZROWS, ZROWS, ZROWS)], rz.at[k - 1], z_s, z_r, k - 1, peersz[k - 1]) for k in range(1, 8)],
        lambda: convolve(2),
    )
    level_rows = rows(z * ZROWS, ZROWS, ZROWS)
    total = red2[level_rows]
    for k in range(7):
        total = total + rz[k]
    zsum[...] = total / scale
    gz[level_rows] = zsum[...]
    run(
        [remote(zsum, gz.at[level_rows], gz_s, gz_r, k - 1, peersz[k - 1]) for k in range(1, 8)],
        lambda: convolve(3),
    )
    spot2 = rows(mine + me1 * PART1 + me2 * PART2, PART2, PART2)
    full[spot2] = gz[0:PART2]
    run([remote(full.at[spot2], full.at[spot2], gb_s, gb_r, k - 1, peers2[k - 1]) for k in range(1, 4)])
    spot1 = rows(mine + me1 * PART1, PART1, PART1)
    run([remote(full.at[spot1], full.at[spot1], ga_s, ga_r, k - 1, peers1[k - 1]) for k in range(1, 4)])
    spot0 = rows(mine, OWN, OWN)
    run([remote(full.at[spot0], full.at[spot0], gc_s, gc_r, 0, partner)])
    final = pltpu.make_async_copy(full.at[0 : 27 * CH], wg_hbm, o_sem.at[2, 0])
    final.start()
    for w in range(2):
        for s in range(BRICKS):
            output_copy(w, s).wait()
    final.wait()


def solution(mesh):
    n_gx = mesh.shape["gx"]
    n_gy = mesh.shape["gy"]

    def local(features, out_grad, kernel, voxel_mask, neighbours, face_sends, edge_sends):
        scale = math.sqrt(n_gx * n_gy * BRICKS * 512)
        vmem = pl.BlockSpec(memory_space=pltpu.VMEM)
        smem = pl.BlockSpec(memory_space=pltpu.SMEM)
        anywhere = pl.BlockSpec(memory_space=pl.ANY)
        dma = pltpu.SemaphoreType.DMA
        brick = (8, 8, 8, CH)
        output, input_grad, weight = pl.pallas_call(
            lambda *refs: step_kernel(n_gx, n_gy, scale, *refs),
            out_shape=(
                jax.ShapeDtypeStruct((BRICKS,) + brick, BF16),
                jax.ShapeDtypeStruct((BRICKS,) + brick, BF16),
                jax.ShapeDtypeStruct((27 * CH, CH), F32),
            ),
            in_specs=[vmem, vmem, vmem, vmem, smem, smem, smem],
            out_specs=(anywhere, anywhere, anywhere),
            scratch_shapes=[
                pltpu.VMEM((BRICKS + 1, 2) + brick, BF16),
                pltpu.VMEM((BRICKS,) + brick, F32),
                pltpu.VMEM((2, 17, 2, 8, 8, CH), BF16),
                pltpu.VMEM((2, 17, 2, 8, 8, CH), BF16),
                pltpu.VMEM((4, 17, 2, 8, CH), BF16),
                pltpu.VMEM((2, 2, 2, 8, 8, CH), BF16),
                pltpu.VMEM((2, 2, 2, 8, 8, CH), BF16),
                pltpu.VMEM((4, 1, 2, 8, CH), BF16),
                pltpu.VMEM((2, BRICKS, 10, 80, 3 * CH), BF16),
                pltpu.VMEM((2, BRICKS, 10, 64, 3 * CH), BF16),
                pltpu.VMEM((BRICKS, CH, 512), BF16),
                pltpu.VMEM((2, 9, 3 * CH, CH), BF16),
                pltpu.VMEM((512, CH), F32),
                pltpu.VMEM((2, BRICKS) + brick, BF16),
                pltpu.VMEM((2 * OWN, CH), F32),
                pltpu.VMEM((OWN, CH), F32),
                pltpu.VMEM((OWN, CH), F32),
                pltpu.VMEM((3, PART1, CH), F32),
                pltpu.VMEM((PART1, CH), F32),
                pltpu.VMEM((3, PART2, CH), F32),
                pltpu.VMEM((8 * ZROWS, CH), F32),
                pltpu.VMEM((7, ZROWS, CH), F32),
                pltpu.VMEM((ZROWS, CH), F32),
                pltpu.VMEM((8 * ZROWS, CH), F32),
                pltpu.VMEM((2 * OWN, CH), F32),
                dma((8,)), dma((8,)),
                dma((1,)), dma((1,)), dma((3,)), dma((3,)), dma((3,)), dma((3,)), dma((7,)), dma((7,)),
                dma((1,)), dma((1,)), dma((3,)), dma((3,)), dma((3,)), dma((3,)), dma((7,)), dma((7,)),
                dma((3, BRICKS)),
            ],
            compiler_params=pltpu.CompilerParams(collective_id=0, has_side_effects=True),
            name="step",
        )(features, out_grad, kernel, voxel_mask, neighbours, face_sends, edge_sends)
        return output, input_grad, weight.reshape(27, CH, CH)

    return jax.shard_map(
        local,
        mesh=mesh,
        in_specs=(
            P(("gx", "gy"), None, None, None, None),
            P(("gx", "gy"), None, None, None, None),
            P(),
            P(("gx", "gy"), None),
            P(("gx", "gy"), None),
            P(("gx", "gy"), None),
            P(("gx", "gy"), None),
        ),
        out_specs=(
            P(("gx", "gy"), None, None, None, None),
            P(("gx", "gy"), None, None, None, None),
            P(),
        ),
        check_vma=False,
    )
```

```python
import math

import jax
import jax.numpy as jnp
from jax import lax
from jax.experimental import pallas as pl
from jax.experimental.pallas import tpu as pltpu
from jax.sharding import PartitionSpec as P

MESH = pl.DeviceIdType.MESH
FACES = ((-1, 0), (1, 0), (0, -1), (0, 1))
EDGES = ((-1, -1), (-1, 1), (1, -1), (1, 1))
TOWARD = FACES + EDGES
CH = 128
BRICKS = 4
OWN = 1792
PART1 = OWN // 4
PART2 = PART1 // 4
ZROWS = 16
HALF = PART1 // 2
F32 = jnp.float32
BF16 = jnp.bfloat16


def step_kernel(
    n_gx, n_gy, scale,
    feat, ograd, kern_hbm, vmask, nbr, fsend, esend,
    outv, igv, full,
    raw, kern, act, maskf, xt, yt, ct, ox, oy, oc, cols, gt, w2, acc,
    part, rc, red, rl, rd, rb, red1, r2, red2, rz, zsum, gz,
    in_s, halo_s, halo_r, c_s, c_r, a_s, a_r, b_s, b_r, z_s, z_r,
    gc_s, gc_r, ga_s, ga_r, gb_s, gb_r, gz_s, gz_r,
):
    loads = [
        pltpu.make_async_copy(feat, raw.at[0], in_s.at[0]),
        pltpu.make_async_copy(ograd, raw.at[1], in_s.at[1]),
        pltpu.make_async_copy(kern_hbm, kern, in_s.at[2]),
    ]
    for load in loads:
        load.start()

    a = lax.axis_index("gx")
    b = lax.axis_index("gy")
    z = a // 2
    y = b // 4
    x = (a % 2) * 2 + (b // 2) % 2
    core = b % 2

    def device(x_, y_, z_, c_):
        return (z_ * 2 + x_ // 2, y_ * 4 + (x_ % 2) * 2 + c_)

    me1 = x + core * (y - x)
    me2 = y + core * (x - y)

    def peer1(p):
        return device(x + (1 - core) * (p - x), y + core * (p - y), z, core)

    def peer2(p):
        return device(x + core * (p - x), y + (1 - core) * (p - y), z, core)

    def exists(d):
        return (a + d[0] >= 0) & (a + d[0] < n_gx) & (b + d[1] >= 0) & (b + d[1] < n_gy)

    partner = device(x, y, z, 1 - core)
    right = peer1((me1 + 1) % 4)
    left = peer1((me1 + 3) % 4)
    peers2 = [peer2((me2 + k) % 4) for k in range(1, 4)]
    peersz = [device(x, y, (z + k) % 8, core) for k in range(1, 8)]

    barrier = pltpu.get_barrier_semaphore()
    for peer in [partner, right, left] + peers2 + peersz:
        pl.semaphore_signal(barrier, inc=1, device_id=peer, device_id_type=MESH)
    expected = 13
    for d in TOWARD:
        there = exists(d)
        expected = expected + there.astype(jnp.int32)

        @pl.when(there)
        def _():
            pl.semaphore_signal(barrier, inc=1, device_id=(a + d[0], b + d[1]), device_id_type=MESH)

    for s in range(BRICKS):
        for g in range(4):
            row = vmask[s : s + 1, g * 128 : (g + 1) * 128].astype(F32)
            tile = jnp.broadcast_to(row, (128, 128)).T
            maskf[s, 2 * g : 2 * g + 2] = tile.reshape(2, 8, 8, CH)

    def far(step):
        return 7 if step > 0 else 0

    loads[0].wait()
    loads[1].wait()
    for i, d in enumerate(TOWARD):
        for j in range(2 if i < 4 else 1):
            entry = fsend[j, i] if i < 4 else esend[j, i - 4]
            spot = jnp.minimum(entry, BRICKS - 1)
            live = (entry < BRICKS).astype(F32)
            for w in range(2):
                if i < 2:
                    keep = maskf[spot, far(d[0])] * live
                    ox[i, j, w] = (raw[w, spot, far(d[0])].astype(F32) * keep).astype(BF16)
                elif i < 4:
                    keep = maskf[spot, :, far(d[1])] * live
                    oy[i - 2, j, w] = (raw[w, spot, :, far(d[1])].astype(F32) * keep).astype(BF16)
                else:
                    keep = maskf[spot, far(d[0]), far(d[1])] * live
                    oc[i - 4, j, w] = (raw[w, spot, far(d[0]), far(d[1])].astype(F32) * keep).astype(BF16)

    def landing(d):
        e = (-d[0], -d[1])
        k = TOWARD.index(e)
        if k < 2:
            return xt.at[k, pl.ds(4 + 2 * k, 2)]
        if k < 4:
            return yt.at[k - 2, pl.ds(4 + 2 * k, 2)]
        return ct.at[k - 4, pl.ds(12 + k - 4, 1)]

    def halo_copy(i):
        d = TOWARD[i]
        source = ox.at[i] if i < 2 else (oy.at[i - 2] if i < 4 else oc.at[i - 4])
        return pltpu.make_async_remote_copy(
            src_ref=source, dst_ref=landing(d), send_sem=halo_s.at[i], recv_sem=halo_r.at[i],
            device_id=(a + d[0], b + d[1]), device_id_type=MESH,
        )

    pl.semaphore_wait(barrier, expected)
    for i, d in enumerate(TOWARD):
        @pl.when(exists(d))
        def _():
            halo_copy(i).start()

        @pl.when(jnp.logical_not(exists((-d[0], -d[1]))))
        def _():
            spot = landing(d)
            spot[...] = jnp.zeros(spot.shape, BF16)

    level = lax.broadcasted_iota(jnp.int32, (1, 8, CH), 1)

    def place(k):
        return slice(k * CH, (k + 1) * CH)

    @pl.loop(0, BRICKS)
    def _(s):
        @pl.loop(0, 8)
        def _(i):
            m = maskf[s, i]
            for w in range(2):
                mid = raw[w, s, i].astype(F32) * m
                act[s, w, i] = mid.astype(BF16)
                down = jnp.where(level == 0, 0.0, pltpu.roll(mid, 1, 1))
                up = jnp.where(level == 7, 0.0, pltpu.roll(mid, 7, 1))
                for k, value in enumerate((down, mid, up)):
                    inner = value[1:7].reshape(48, CH).astype(BF16)
                    cols[w, s, i + 1, 0, 16:64, place(k)] = inner
                    cols[w, s, i + 1, 1, :, place(k)] = value.reshape(64, CH).astype(BF16)
                    cols[w, s, i + 1, 2, 0:48, place(k)] = inner

    for side in range(2):
        xt[side, 16] = jnp.zeros((2, 8, 8, CH), BF16)
        yt[side, 16] = jnp.zeros((2, 8, 8, CH), BF16)
    for corner in range(4):
        ct[corner, 16] = jnp.zeros((2, 8, CH), BF16)
    for s in range(BRICKS):
        for side in range(2):
            xt[side, s] = act[s, :, 7 - 7 * side]
            yt[side, s] = act[s, :, :, 7 - 7 * side]
        for corner, e in enumerate(EDGES):
            ct[corner, s] = act[s, :, far(-e[0]), far(-e[1])]

    @pl.loop(0, BRICKS)
    def _(s):
        for g in range(4):
            rows_ = act[s, 1, 2 * g : 2 * g + 2].astype(F32).reshape(128, CH)
            gt[s, :, g * 128 : (g + 1) * 128] = rows_.T.astype(BF16)

    part[27 * CH : 28 * CH] = jnp.zeros((CH, CH), F32)
    red2[PART2 : 8 * ZROWS] = jnp.zeros((8 * ZROWS - PART2, CH), F32)

    for i, d in enumerate(TOWARD):
        @pl.when(exists(d))
        def _():
            halo_copy(i).wait_send()

        @pl.when(exists((-d[0], -d[1])))
        def _():
            halo_copy(i).wait_recv()

    for corner, e in enumerate(EDGES):
        side_x = (e[0] + 1) // 2
        side_y = (e[1] + 1) // 2
        for j in range(2):
            ct[corner, 4 + 2 * side_x + j] = xt[side_x, 4 + 2 * side_x + j, :, far(-e[1])]
            ct[corner, 8 + 2 * side_y + j] = yt[side_y, 8 + 2 * side_y + j, :, far(-e[0])]

    def shifted(below, here, above):
        down = jnp.where(level == 0, pltpu.roll(below, 1, 1), pltpu.roll(here, 1, 1))
        up = jnp.where(level == 7, pltpu.roll(above, 7, 1), pltpu.roll(here, 7, 1))
        return down, here, up

    def outer_columns(w):
        @pl.loop(0, BRICKS)
        def _(s):
            for side in range(2):
                column = 18 * side
                mids = [xt[side, nbr[s, column + 3 + k], w].astype(F32) for k in range(3)]
                lows = [ct[2 * side, nbr[s, column + k], w].astype(F32).reshape(1, 8, CH) for k in range(3)]
                highs = [ct[2 * side + 1, nbr[s, column + 6 + k], w].astype(F32).reshape(1, 8, CH) for k in range(3)]
                whole = [jnp.concatenate([lows[k], mids[k], highs[k]], axis=0) for k in range(3)]
                for k, value in enumerate(shifted(*whole)):
                    for q in range(3):
                        cols[w, s, 9 * side, q, :, place(k)] = value[q : q + 8].reshape(64, CH).astype(BF16)

            low_at = [nbr[s, 9 + k] for k in range(3)]
            high_at = [nbr[s, 15 + k] for k in range(3)]

            @pl.loop(0, 8)
            def _(i):
                first = act[s, w, i, 0].astype(F32).reshape(1, 8, CH)
                last = act[s, w, i, 7].astype(F32).reshape(1, 8, CH)
                zero = jnp.zeros((1, 8, CH), F32)
                lows = [yt[0, low_at[k], w, i].astype(F32).reshape(1, 8, CH) for k in range(3)]
                highs = [yt[1, high_at[k], w, i].astype(F32).reshape(1, 8, CH) for k in range(3)]
                inner = [(zero, zero), (first, last), (zero, zero)]
                whole = [jnp.concatenate([lows[k], inner[k][0], inner[k][1], highs[k]], axis=0) for k in range(3)]
                for k, value in enumerate(shifted(*whole)):
                    cols[w, s, i + 1, 0, 0:16, place(k)] = value[0:2].reshape(16, CH).astype(BF16)
                    cols[w, s, i + 1, 2, 48:64, place(k)] = value[2:4].reshape(16, CH).astype(BF16)

    outer_columns(0)

    def columns(w, s, first, k):
        return cols[w, s, pl.ds(first, 8), k].reshape(512, 3 * CH)

    def weight_unit(i):
        u = i + (1 - core) * (8 - 2 * i)
        n = u // 3
        k = u % 3
        total = jnp.dot(gt[0], columns(0, 0, n, k), preferred_element_type=F32)
        for s in range(1, BRICKS):
            total = total + jnp.dot(gt[s], columns(0, s, n, k), preferred_element_type=F32)
        for q in range(3):
            part[pl.ds(pl.multiple_of((3 * u + q) * CH, CH), CH)] = total[:, place(q)].T

    def convolve(s):
        @pl.loop(0, 2)
        def _(w):
            for first in range(3):
                value = jnp.concatenate([columns(w, s, first, k) for k in range(3)], axis=1)
                weight = w2[w, 3 * first : 3 * first + 3].reshape(9 * CH, CH)
                term = jnp.dot(value, weight, preferred_element_type=F32)
                if first == 0:
                    acc[...] = term
                elif first == 1:
                    acc[...] += term
                else:
                    term = (acc[...] + term) * maskf[s].reshape(512, CH)
                    result = term.reshape(8, 8, 8, CH).astype(BF16)

                    @pl.when(w == 0)
                    def _():
                        outv[s] = result

                    @pl.when(w == 1)
                    def _():
                        igv[s] = result

    def remote(source, target, sems, semr, k, peer):
        return pltpu.make_async_remote_copy(
            src_ref=source, dst_ref=target, send_sem=sems.at[k], recv_sem=semr.at[k],
            device_id=peer, device_id_type=MESH,
        )

    def start(copies):
        for copy in copies:
            copy.start()
        return copies

    def finish(copies):
        for copy in copies:
            copy.wait()

    def rows(start, size, unit):
        return pl.ds(pl.multiple_of(start, unit), size)

    mine = core * OWN
    other = (1 - core) * OWN
    order = (2, 1, 3, 0)

    def chunk(p):
        return rows(p % 4 * PART1, PART1, PART1)

    def half(p, which):
        return rows(p % 4 * PART1 + which * HALF, HALF, HALF)

    @pl.loop(0, 5)
    def _(i):
        weight_unit(i)

    pair = start([
        remote(part.at[rows(other + (me2 + k) % 4 * PART1, PART1, PART1)], rc.at[chunk(me2 + k)], c_s, c_r, j, partner)
        for j, k in enumerate(order)
    ])

    @pl.loop(5, 9)
    def _(i):
        weight_unit(i)

    def settle(j):
        pair[j].wait()
        base = (me1 + order[j]) % 4 * PART1

        @pl.loop(0, PART1 // 64)
        def _(i):
            red[rows(base + i * 64, 64, 64)] = part[rows(mine + base + i * 64, 64, 64)] + rc[rows(base + i * 64, 64, 64)]

    settle(0)
    relay_a = remote(red.at[half(me1 + 2, 0)], rl.at[0], a_s, a_r, 0, right)
    relay_b = remote(red.at[half(me1 + 2, 1)], rl.at[1], a_s, a_r, 1, left)
    start([relay_a, relay_b])
    settle(1)
    direct_b = remote(red.at[half(me1 + 1, 1)], rd.at[1], a_s, a_r, 2, right)
    start([direct_b])
    settle(2)
    direct_a = remote(red.at[half(me1 + 3, 0)], rd.at[0], a_s, a_r, 3, left)
    start([direct_a])
    settle(3)

    loads[2].wait()

    @pl.loop(0, 9)
    def _(n):
        for k in range(3):
            w2[0, n, k * CH : (k + 1) * CH] = kern[3 * n + k]
            w2[1, n, k * CH : (k + 1) * CH] = kern[26 - 3 * n - k].astype(F32).T.astype(BF16)

    outer_columns(1)

    def join(p, which):
        at = half(p, which)
        red[at] = red[at] + rl[which]

    relay_a.wait()
    join(me1 + 1, 0)
    joined_a = remote(red.at[half(me1 + 1, 0)], rb.at[0], a_s, a_r, 4, right)
    start([joined_a])
    relay_b.wait()
    join(me1 + 3, 1)
    joined_b = remote(red.at[half(me1 + 3, 1)], rb.at[1], a_s, a_r, 5, left)
    start([joined_b])
    convolve(0)
    finish([direct_a, direct_b, joined_a, joined_b])
    for which in range(2):
        red1[which * HALF : (which + 1) * HALF] = red[half(me1, which)] + rd[which] + rb[which]

    second = start([
        remote(red1.at[rows((me2 + k) % 4 * PART2, PART2, PART2)], r2.at[k - 1], b_s, b_r, k - 1, peers2[k - 1])
        for k in range(1, 4)
    ])
    convolve(1)
    finish(second)
    red2[0:PART2] = red1[rows(me2 * PART2, PART2, PART2)] + r2[0] + r2[1] + r2[2]
    third = start([
        remote(red2.at[rows((z + k) % 8 * ZROWS, ZROWS, ZROWS)], rz.at[k - 1], z_s, z_r, k - 1, peersz[k - 1])
        for k in range(1, 8)
    ])
    convolve(2)
    finish(third)
    level_rows = rows(z * ZROWS, ZROWS, ZROWS)
    total = red2[level_rows]
    for k in range(7):
        total = total + rz[k]
    zsum[...] = total / scale
    gz[level_rows] = zsum[...]
    fourth = start([remote(zsum, gz.at[level_rows], gz_s, gz_r, k - 1, peersz[k - 1]) for k in range(1, 8)])
    convolve(3)
    finish(fourth)
    spot2 = rows(mine + me1 * PART1 + me2 * PART2, PART2, PART2)
    full[spot2] = gz[0:PART2]
    finish(start([remote(full.at[spot2], full.at[spot2], gb_s, gb_r, k - 1, peers2[k - 1]) for k in range(1, 4)]))

    def share(p, which, k, peer):
        at = rows(mine + p % 4 * PART1 + which * HALF, HALF, HALF)
        return remote(full.at[at], full.at[at], ga_s, ga_r, k, peer)

    def hand(p, j):
        at = rows(mine + p % 4 * PART1, PART1, PART1)
        return remote(full.at[at], full.at[at], gc_s, gc_r, j, partner)

    own_a = share(me1, 0, 0, right)
    own_b = share(me1, 1, 1, left)
    rest_b = share(me1, 1, 2, right)
    rest_a = share(me1, 0, 3, left)
    start([own_a, own_b, rest_b, rest_a])
    hands = start([hand(me1, 0)])
    own_a.wait()
    on_a = share(me1 + 3, 0, 4, right)
    on_a.start()
    own_b.wait()
    on_b = share(me1 + 1, 1, 5, left)
    on_b.start()
    rest_b.wait()
    hands += start([hand(me1 + 3, 1)])
    rest_a.wait()
    hands += start([hand(me1 + 1, 2)])
    finish([on_a, on_b])
    hands += start([hand(me1 + 2, 3)])
    finish(hands)


def store_kernel(outv, igv, full, out_hbm, ig_hbm, wg_hbm, sem):
    copies = [
        pltpu.make_async_copy(full.at[0 : 27 * CH], wg_hbm, sem.at[0]),
        pltpu.make_async_copy(outv, out_hbm, sem.at[1]),
        pltpu.make_async_copy(igv, ig_hbm, sem.at[2]),
    ]
    for copy in copies:
        copy.start()
    for copy in copies:
        copy.wait()


def solution(mesh):
    n_gx = mesh.shape["gx"]
    n_gy = mesh.shape["gy"]

    def local(features, out_grad, kernel, voxel_mask, neighbours, face_sends, edge_sends):
        scale = math.sqrt(n_gx * n_gy * BRICKS * 512)
        vmem = pl.BlockSpec(memory_space=pltpu.VMEM)
        smem = pl.BlockSpec(memory_space=pltpu.SMEM)
        anywhere = pl.BlockSpec(memory_space=pl.ANY)
        dma = pltpu.SemaphoreType.DMA
        brick = (8, 8, 8, CH)
        held = pl.pallas_call(
            lambda *refs: step_kernel(n_gx, n_gy, scale, *refs),
            out_shape=(
                pltpu.VMEM((BRICKS,) + brick, BF16),
                pltpu.VMEM((BRICKS,) + brick, BF16),
                pltpu.VMEM((2 * OWN, CH), F32),
            ),
            in_specs=[anywhere, anywhere, anywhere, vmem, smem, smem, smem],
            out_specs=(vmem, vmem, vmem),
            scratch_shapes=[
                pltpu.VMEM((2, BRICKS) + brick, BF16),
                pltpu.VMEM((27, CH, CH), BF16),
                pltpu.VMEM((BRICKS, 2) + brick, BF16),
                pltpu.VMEM((BRICKS,) + brick, F32),
                pltpu.VMEM((2, 17, 2, 8, 8, CH), BF16),
                pltpu.VMEM((2, 17, 2, 8, 8, CH), BF16),
                pltpu.VMEM((4, 17, 2, 8, CH), BF16),
                pltpu.VMEM((2, 2, 2, 8, 8, CH), BF16),
                pltpu.VMEM((2, 2, 2, 8, 8, CH), BF16),
                pltpu.VMEM((4, 1, 2, 8, CH), BF16),
                pltpu.VMEM((2, BRICKS, 10, 3, 64, 3 * CH), BF16),
                pltpu.VMEM((BRICKS, CH, 512), BF16),
                pltpu.VMEM((2, 9, 3 * CH, CH), BF16),
                pltpu.VMEM((512, CH), F32),
                pltpu.VMEM((2 * OWN, CH), F32),
                pltpu.VMEM((OWN, CH), F32),
                pltpu.VMEM((OWN, CH), F32),
                pltpu.VMEM((2, HALF, CH), F32),
                pltpu.VMEM((2, HALF, CH), F32),
                pltpu.VMEM((2, HALF, CH), F32),
                pltpu.VMEM((PART1, CH), F32),
                pltpu.VMEM((3, PART2, CH), F32),
                pltpu.VMEM((8 * ZROWS, CH), F32),
                pltpu.VMEM((7, ZROWS, CH), F32),
                pltpu.VMEM((ZROWS, CH), F32),
                pltpu.VMEM((8 * ZROWS, CH), F32),
                dma((3,)), dma((8,)), dma((8,)),
                dma((4,)), dma((4,)), dma((6,)), dma((6,)), dma((3,)), dma((3,)), dma((7,)), dma((7,)),
                dma((4,)), dma((4,)), dma((6,)), dma((6,)), dma((3,)), dma((3,)), dma((7,)), dma((7,)),
            ],
            compiler_params=pltpu.CompilerParams(collective_id=0, has_side_effects=True),
            name="step",
        )(features, out_grad, kernel, voxel_mask, neighbours, face_sends.T, edge_sends.T)
        output, input_grad, weight = pl.pallas_call(
            store_kernel,
            out_shape=(
                jax.ShapeDtypeStruct((BRICKS,) + brick, BF16),
                jax.ShapeDtypeStruct((BRICKS,) + brick, BF16),
                jax.ShapeDtypeStruct((27 * CH, CH), F32),
            ),
            in_specs=[vmem, vmem, vmem],
            out_specs=(anywhere, anywhere, anywhere),
            scratch_shapes=[dma((3,))],
            name="store",
        )(*(pltpu.with_memory_space_constraint(h, pltpu.VMEM) for h in held))
        return output, input_grad, weight.reshape(27, CH, CH)

    return jax.shard_map(
        local,
        mesh=mesh,
        in_specs=(
            P(("gx", "gy"), None, None, None, None),
            P(("gx", "gy"), None, None, None, None),
            P(),
            P(("gx", "gy"), None),
            P(("gx", "gy"), None),
            P(("gx", "gy"), None),
            P(("gx", "gy"), None),
        ),
        out_specs=(
            P(("gx", "gy"), None, None, None, None),
            P(("gx", "gy"), None, None, None, None),
            P(),
        ),
        check_vma=False,
    )
```

```python
import math

import jax
import jax.numpy as jnp
from jax import lax
from jax.experimental import pallas as pl
from jax.experimental.pallas import tpu as pltpu
from jax.sharding import PartitionSpec as P

MESH = pl.DeviceIdType.MESH
FACES = ((-1, 0), (1, 0), (0, -1), (0, 1))
EDGES = ((-1, -1), (-1, 1), (1, -1), (1, 1))
TOWARD = FACES + EDGES
CH = 128
BRICKS = 4
OWN = 1792
HALF = OWN // 2
PART1 = HALF // 4
PART2 = PART1 // 4
ZROWS = 16
F32 = jnp.float32
BF16 = jnp.bfloat16


def step_kernel(
    n_gx, n_gy, scale,
    feat, ograd, kern_hbm, vmask, nbr, fsend, esend,
    outv, igv, full,
    raw_a, raw_g, kern, act, maskf, xt_a, xt_g, yt_a, yt_g, ct_a, ct_g, ox, oy, oc, cols, gt, w2, acc,
    part, rc, red, r1, red1, r2, red2, rz, zsum, gz,
    in_s, halo_s, halo_r, c_s, c_r, a_s, a_r, b_s, b_r, z_s, z_r,
    gc_s, gc_r, ga_s, ga_r, gb_s, gb_r, gz_s, gz_r,
):
    raw, xt, yt, ct = (raw_a, raw_g), (xt_a, xt_g), (yt_a, yt_g), (ct_a, ct_g)
    loads = [
        pltpu.make_async_copy(feat, raw_a, in_s.at[0]),
        pltpu.make_async_copy(ograd, raw_g, in_s.at[1]),
        pltpu.make_async_copy(kern_hbm, kern, in_s.at[2]),
    ]
    for load in loads:
        load.start()

    a = lax.axis_index("gx")
    b = lax.axis_index("gy")
    z = a // 2
    y = b // 4
    x = (a % 2) * 2 + (b // 2) % 2
    core = b % 2

    def device(x_, y_, z_, c_):
        return (z_ * 2 + x_ // 2, y_ * 4 + (x_ % 2) * 2 + c_)

    first_at = (x, y)
    second_at = (y, x)

    def peer_x(k):
        return device((x + k) % 4, y, z, core)

    def peer_y(k):
        return device(x, (y + k) % 4, z, core)

    def exists(d):
        return (a + d[0] >= 0) & (a + d[0] < n_gx) & (b + d[1] >= 0) & (b + d[1] < n_gy)

    partner = device(x, y, z, 1 - core)
    near = ([peer_x(k) for k in range(1, 4)], [peer_y(k) for k in range(1, 4)])
    peersz = [device(x, y, (z + k) % 8, core) for k in range(1, 8)]

    barrier = pltpu.get_barrier_semaphore()
    for peer in [partner] + near[0] + near[1] + peersz:
        pl.semaphore_signal(barrier, inc=1, device_id=peer, device_id_type=MESH)
    expected = 14
    for d in TOWARD:
        there = exists(d)
        expected = expected + there.astype(jnp.int32)

        @pl.when(there)
        def _():
            pl.semaphore_signal(barrier, inc=1, device_id=(a + d[0], b + d[1]), device_id_type=MESH)

    for s in range(BRICKS):
        for g in range(4):
            row = vmask[s : s + 1, g * 128 : (g + 1) * 128].astype(F32)
            tile = jnp.broadcast_to(row, (128, 128)).T
            maskf[s, 2 * g : 2 * g + 2] = tile.reshape(2, 8, 8, CH)

    def far(step):
        return 7 if step > 0 else 0

    def gather_rims(w):
        for i, d in enumerate(TOWARD):
            for j in range(2 if i < 4 else 1):
                entry = fsend[j, i] if i < 4 else esend[j, i - 4]
                spot = jnp.minimum(entry, BRICKS - 1)
                live = (entry < BRICKS).astype(F32)
                if i < 2:
                    keep = maskf[spot, far(d[0])] * live
                    ox[i, w, j] = (raw[w][spot, far(d[0])].astype(F32) * keep).astype(BF16)
                elif i < 4:
                    keep = maskf[spot, :, far(d[1])] * live
                    oy[i - 2, w, j] = (raw[w][spot, :, far(d[1])].astype(F32) * keep).astype(BF16)
                else:
                    keep = maskf[spot, far(d[0]), far(d[1])] * live
                    oc[i - 4, w, j] = (raw[w][spot, far(d[0]), far(d[1])].astype(F32) * keep).astype(BF16)

    def landing(d, w):
        e = (-d[0], -d[1])
        k = TOWARD.index(e)
        if k < 2:
            return xt[w].at[k, pl.ds(4 + 2 * k, 2)]
        if k < 4:
            return yt[w].at[k - 2, pl.ds(4 + 2 * k, 2)]
        return ct[w].at[k - 4, pl.ds(12 + k - 4, 1)]

    def halo_copy(i, w):
        d = TOWARD[i]
        source = ox.at[i, w] if i < 2 else (oy.at[i - 2, w] if i < 4 else oc.at[i - 4, w])
        return pltpu.make_async_remote_copy(
            src_ref=source, dst_ref=landing(d, w), send_sem=halo_s.at[w, i], recv_sem=halo_r.at[w, i],
            device_id=(a + d[0], b + d[1]), device_id_type=MESH,
        )

    def send_rims(w):
        for i, d in enumerate(TOWARD):
            @pl.when(exists(d))
            def _():
                halo_copy(i, w).start()

    def await_rims(w):
        for i, d in enumerate(TOWARD):
            @pl.when(exists(d))
            def _():
                halo_copy(i, w).wait_send()

            @pl.when(exists((-d[0], -d[1])))
            def _():
                halo_copy(i, w).wait_recv()

        for corner, e in enumerate(EDGES):
            side_x = (e[0] + 1) // 2
            side_y = (e[1] + 1) // 2
            for j in range(2):
                ct[w][corner, 4 + 2 * side_x + j] = xt[w][side_x, 4 + 2 * side_x + j, far(-e[1])]
                ct[w][corner, 8 + 2 * side_y + j] = yt[w][side_y, 8 + 2 * side_y + j, far(-e[0])]

    loads[0].wait()
    gather_rims(0)
    pl.semaphore_wait(barrier, expected)
    send_rims(0)
    loads[1].wait()
    gather_rims(1)

    for d in TOWARD:
        @pl.when(jnp.logical_not(exists((-d[0], -d[1]))))
        def _():
            for w in range(2):
                spot = landing(d, w)
                spot[...] = jnp.zeros(spot.shape, BF16)

    level = lax.broadcasted_iota(jnp.int32, (1, 8, CH), 1)

    def place(k):
        return slice(k * CH, (k + 1) * CH)

    @pl.loop(0, BRICKS)
    def _(s):
        @pl.loop(0, 8)
        def _(i):
            m = maskf[s, i]
            for w in range(2):
                mid = raw[w][s, i].astype(F32) * m
                act[w, s, i] = mid.astype(BF16)
                down = jnp.where(level == 0, 0.0, pltpu.roll(mid, 1, 1))
                up = jnp.where(level == 7, 0.0, pltpu.roll(mid, 7, 1))
                for k, value in enumerate((down, mid, up)):
                    inner = value[1:7].reshape(48, CH).astype(BF16)
                    cols[w, s, i + 1, 0, 16:64, place(k)] = inner
                    cols[w, s, i + 1, 1, :, place(k)] = value.reshape(64, CH).astype(BF16)
                    cols[w, s, i + 1, 2, 0:48, place(k)] = inner

    for w in range(2):
        for side in range(2):
            xt[w][side, 16] = jnp.zeros((8, 8, CH), BF16)
            yt[w][side, 16] = jnp.zeros((8, 8, CH), BF16)
            for s in range(BRICKS):
                xt[w][side, s] = act[w, s, 7 - 7 * side]
                yt[w][side, s] = act[w, s, :, 7 - 7 * side]
        for corner, e in enumerate(EDGES):
            ct[w][corner, 16] = jnp.zeros((8, CH), BF16)
            for s in range(BRICKS):
                ct[w][corner, s] = act[w, s, far(-e[0]), far(-e[1])]

    @pl.loop(0, BRICKS)
    def _(s):
        for g in range(4):
            rows_ = act[1, s, 2 * g : 2 * g + 2].astype(F32).reshape(128, CH)
            gt[s, :, g * 128 : (g + 1) * 128] = rows_.T.astype(BF16)

    part[27 * CH : 28 * CH] = jnp.zeros((CH, CH), F32)
    red2[2 * PART2 : 8 * ZROWS] = jnp.zeros((8 * ZROWS - 2 * PART2, CH), F32)

    await_rims(0)
    send_rims(1)

    def shifted(below, here, above):
        down = jnp.where(level == 0, pltpu.roll(below, 1, 1), pltpu.roll(here, 1, 1))
        up = jnp.where(level == 7, pltpu.roll(above, 7, 1), pltpu.roll(here, 7, 1))
        return down, here, up

    def outer_columns(w):
        @pl.loop(0, BRICKS)
        def _(s):
            for side in range(2):
                column = 18 * side
                mids = [xt[w][side, nbr[s, column + 3 + k]].astype(F32) for k in range(3)]
                lows = [ct[w][2 * side, nbr[s, column + k]].astype(F32).reshape(1, 8, CH) for k in range(3)]
                highs = [ct[w][2 * side + 1, nbr[s, column + 6 + k]].astype(F32).reshape(1, 8, CH) for k in range(3)]
                whole = [jnp.concatenate([lows[k], mids[k], highs[k]], axis=0) for k in range(3)]
                for k, value in enumerate(shifted(*whole)):
                    for q in range(3):
                        cols[w, s, 9 * side, q, :, place(k)] = value[q : q + 8].reshape(64, CH).astype(BF16)

            low_at = [nbr[s, 9 + k] for k in range(3)]
            high_at = [nbr[s, 15 + k] for k in range(3)]

            @pl.loop(0, 8)
            def _(i):
                first = act[w, s, i, 0].astype(F32).reshape(1, 8, CH)
                last = act[w, s, i, 7].astype(F32).reshape(1, 8, CH)
                zero = jnp.zeros((1, 8, CH), F32)
                lows = [yt[w][0, low_at[k], i].astype(F32).reshape(1, 8, CH) for k in range(3)]
                highs = [yt[w][1, high_at[k], i].astype(F32).reshape(1, 8, CH) for k in range(3)]
                inner = [(zero, zero), (first, last), (zero, zero)]
                whole = [jnp.concatenate([lows[k], inner[k][0], inner[k][1], highs[k]], axis=0) for k in range(3)]
                for k, value in enumerate(shifted(*whole)):
                    cols[w, s, i + 1, 0, 0:16, place(k)] = value[0:2].reshape(16, CH).astype(BF16)
                    cols[w, s, i + 1, 2, 48:64, place(k)] = value[2:4].reshape(16, CH).astype(BF16)

    outer_columns(0)

    def columns(w, s, first, k):
        return cols[w, s, pl.ds(first, 8), k].reshape(512, 3 * CH)

    def weight_unit(i):
        u = i + (1 - core) * (8 - 2 * i)
        n = u // 3
        k = u % 3
        total = jnp.dot(gt[0], columns(0, 0, n, k), preferred_element_type=F32)
        for s in range(1, BRICKS):
            total = total + jnp.dot(gt[s], columns(0, s, n, k), preferred_element_type=F32)
        for q in range(3):
            part[pl.ds(pl.multiple_of((3 * u + q) * CH, CH), CH)] = total[:, place(q)].T

    def convolve(s):
        @pl.loop(0, 2)
        def _(w):
            for first in range(3):
                value = jnp.concatenate([columns(w, s, first, k) for k in range(3)], axis=1)
                weight = w2[w, 3 * first : 3 * first + 3].reshape(9 * CH, CH)
                term = jnp.dot(value, weight, preferred_element_type=F32)
                if first == 0:
                    acc[...] = term
                elif first == 1:
                    acc[...] += term
                else:
                    term = (acc[...] + term) * maskf[s].reshape(512, CH)
                    result = term.reshape(8, 8, 8, CH).astype(BF16)

                    @pl.when(w == 0)
                    def _():
                        outv[s] = result

                    @pl.when(w == 1)
                    def _():
                        igv[s] = result

    def remote(source, target, sems, semr, k, peer):
        return pltpu.make_async_remote_copy(
            src_ref=source, dst_ref=target, send_sem=sems.at[k], recv_sem=semr.at[k],
            device_id=peer, device_id_type=MESH,
        )

    def start(copies):
        for copy in copies:
            copy.start()
        return copies

    def finish(copies):
        for copy in copies:
            copy.wait()

    def rows(start, size, unit):
        return pl.ds(pl.multiple_of(start, unit), size)

    mine = core * OWN
    other = (1 - core) * OWN
    order = (2, 1, 3, 0)

    def chunk(h, p, base=0):
        return rows(base + h * HALF + p % 4 * PART1, PART1, PART1)

    @pl.loop(0, 5)
    def _(i):
        weight_unit(i)

    steps = [(k, h) for k in order for h in range(2)]
    pair = start([
        remote(part.at[chunk(h, first_at[h] + k, other)], rc.at[chunk(h, first_at[h] + k)], c_s, c_r, j, partner)
        for j, (k, h) in enumerate(steps)
    ])

    @pl.loop(5, 9)
    def _(i):
        weight_unit(i)

    first = []
    for j, (k, h) in enumerate(steps):
        pair[j].wait()
        base = h * HALF + (first_at[h] + k) % 4 * PART1

        @pl.loop(0, PART1 // 32)
        def _(i):
            at = rows(base + i * 32, 32, 32)
            red[at] = part[rows(mine + base + i * 32, 32, 32)] + rc[at]

        if k:
            first += start([remote(red.at[chunk(h, first_at[h] + k)], r1.at[h, k - 1], a_s.at[h], a_r.at[h], k - 1, near[h][k - 1])])

    loads[2].wait()

    @pl.loop(0, 9)
    def _(n):
        for k in range(3):
            w2[0, n, k * CH : (k + 1) * CH] = kern[3 * n + k]
            w2[1, n, k * CH : (k + 1) * CH] = kern[26 - 3 * n - k].astype(F32).T.astype(BF16)

    await_rims(1)
    outer_columns(1)
    convolve(0)
    finish(first)

    second = []
    for h in range(2):
        @pl.loop(0, PART1 // 32)
        def _(i):
            at = rows(i * 32, 32, 32)
            own = red[rows(h * HALF + first_at[h] * PART1 + i * 32, 32, 32)]
            red1[h, at] = own + r1[h, 0, at] + r1[h, 1, at] + r1[h, 2, at]

        second += start([
            remote(
                red1.at[h, rows((second_at[h] + k) % 4 * PART2, PART2, PART2)], r2.at[h, k - 1],
                b_s.at[h], b_r.at[h], k - 1, near[1 - h][k - 1],
            )
            for k in range(1, 4)
        ])
    convolve(1)
    finish(second)
    for h in range(2):
        own = red1[h, rows(second_at[h] * PART2, PART2, PART2)]
        red2[h * PART2 : (h + 1) * PART2] = own + r2[h, 0] + r2[h, 1] + r2[h, 2]
    third = start([
        remote(red2.at[rows((z + k) % 8 * ZROWS, ZROWS, ZROWS)], rz.at[k - 1], z_s, z_r, k - 1, peersz[k - 1])
        for k in range(1, 8)
    ])
    convolve(2)
    finish(third)
    level_rows = rows(z * ZROWS, ZROWS, ZROWS)
    total = red2[level_rows]
    for k in range(7):
        total = total + rz[k]
    zsum[...] = total / scale
    gz[level_rows] = zsum[...]
    fourth = start([remote(zsum, gz.at[level_rows], gz_s, gz_r, k - 1, peersz[k - 1]) for k in range(1, 8)])
    convolve(3)
    finish(fourth)
    spread = []
    for h in range(2):
        spot2 = rows(mine + h * HALF + first_at[h] * PART1 + second_at[h] * PART2, PART2, PART2)
        full[spot2] = gz[h * PART2 : (h + 1) * PART2]
        spread += start([
            remote(full.at[spot2], full.at[spot2], gb_s.at[h], gb_r.at[h], k - 1, near[1 - h][k - 1])
            for k in range(1, 4)
        ])
    finish(spread)

    def hand(h, k):
        at = chunk(h, first_at[h] + 4 - k, mine)
        return remote(full.at[at], full.at[at], gc_s.at[h], gc_r.at[h], k, partner)

    last = {}
    for k in (2, 1, 3):
        for h in range(2):
            spot1 = chunk(h, first_at[h], mine)
            last[h, k] = remote(full.at[spot1], full.at[spot1], ga_s.at[h], ga_r.at[h], k - 1, near[h][k - 1])
            last[h, k].start()
    hands = start([hand(h, 0) for h in range(2)])
    for k in (1, 3, 2):
        for h in range(2):
            last[h, k].wait()
            hands += start([hand(h, k)])
    finish(hands)


def store_kernel(outv, igv, full, out_hbm, ig_hbm, wg_hbm, sem):
    copies = [
        pltpu.make_async_copy(full.at[0 : 27 * CH], wg_hbm, sem.at[0]),
        pltpu.make_async_copy(outv, out_hbm, sem.at[1]),
        pltpu.make_async_copy(igv, ig_hbm, sem.at[2]),
    ]
    for copy in copies:
        copy.start()
    for copy in copies:
        copy.wait()


def solution(mesh):
    n_gx = mesh.shape["gx"]
    n_gy = mesh.shape["gy"]

    def local(features, out_grad, kernel, voxel_mask, neighbours, face_sends, edge_sends):
        scale = math.sqrt(n_gx * n_gy * BRICKS * 512)
        vmem = pl.BlockSpec(memory_space=pltpu.VMEM)
        smem = pl.BlockSpec(memory_space=pltpu.SMEM)
        anywhere = pl.BlockSpec(memory_space=pl.ANY)
        dma = pltpu.SemaphoreType.DMA
        brick = (8, 8, 8, CH)
        held = pl.pallas_call(
            lambda *refs: step_kernel(n_gx, n_gy, scale, *refs),
            out_shape=(
                pltpu.VMEM((BRICKS,) + brick, BF16),
                pltpu.VMEM((BRICKS,) + brick, BF16),
                pltpu.VMEM((2 * OWN, CH), F32),
            ),
            in_specs=[anywhere, anywhere, anywhere, vmem, smem, smem, smem],
            out_specs=(vmem, vmem, vmem),
            scratch_shapes=[
                pltpu.VMEM((BRICKS,) + brick, BF16),
                pltpu.VMEM((BRICKS,) + brick, BF16),
                pltpu.VMEM((27, CH, CH), BF16),
                pltpu.VMEM((2, BRICKS) + brick, BF16),
                pltpu.VMEM((BRICKS,) + brick, F32),
                pltpu.VMEM((2, 17, 8, 8, CH), BF16),
                pltpu.VMEM((2, 17, 8, 8, CH), BF16),
                pltpu.VMEM((2, 17, 8, 8, CH), BF16),
                pltpu.VMEM((2, 17, 8, 8, CH), BF16),
                pltpu.VMEM((4, 17, 8, CH), BF16),
                pltpu.VMEM((4, 17, 8, CH), BF16),
                pltpu.VMEM((2, 2, 2, 8, 8, CH), BF16),
                pltpu.VMEM((2, 2, 2, 8, 8, CH), BF16),
                pltpu.VMEM((4, 2, 1, 8, CH), BF16),
                pltpu.VMEM((2, BRICKS, 10, 3, 64, 3 * CH), BF16),
                pltpu.VMEM((BRICKS, CH, 512), BF16),
                pltpu.VMEM((2, 9, 3 * CH, CH), BF16),
                pltpu.VMEM((512, CH), F32),
                pltpu.VMEM((2 * OWN, CH), F32),
                pltpu.VMEM((OWN, CH), F32),
                pltpu.VMEM((OWN, CH), F32),
                pltpu.VMEM((2, 3, PART1, CH), F32),
                pltpu.VMEM((2, PART1, CH), F32),
                pltpu.VMEM((2, 3, PART2, CH), F32),
                pltpu.VMEM((8 * ZROWS, CH), F32),
                pltpu.VMEM((7, ZROWS, CH), F32),
                pltpu.VMEM((ZROWS, CH), F32),
                pltpu.VMEM((8 * ZROWS, CH), F32),
                dma((3,)), dma((2, 8)), dma((2, 8)),
                dma((8,)), dma((8,)), dma((2, 3)), dma((2, 3)), dma((2, 3)), dma((2, 3)), dma((7,)), dma((7,)),
                dma((2, 4)), dma((2, 4)), dma((2, 3)), dma((2, 3)), dma((2, 3)), dma((2, 3)), dma((7,)), dma((7,)),
            ],
            compiler_params=pltpu.CompilerParams(collective_id=0, has_side_effects=True),
            name="step",
        )(features, out_grad, kernel, voxel_mask, neighbours, face_sends.T, edge_sends.T)
        output, input_grad, weight = pl.pallas_call(
            store_kernel,
            out_shape=(
                jax.ShapeDtypeStruct((BRICKS,) + brick, BF16),
                jax.ShapeDtypeStruct((BRICKS,) + brick, BF16),
                jax.ShapeDtypeStruct((27 * CH, CH), F32),
            ),
            in_specs=[vmem, vmem, vmem],
            out_specs=(anywhere, anywhere, anywhere),
            scratch_shapes=[dma((3,))],
            name="store",
        )(*(pltpu.with_memory_space_constraint(h, pltpu.VMEM) for h in held))
        return output, input_grad, weight.reshape(27, CH, CH)

    return jax.shard_map(
        local,
        mesh=mesh,
        in_specs=(
            P(("gx", "gy"), None, None, None, None),
            P(("gx", "gy"), None, None, None, None),
            P(),
            P(("gx", "gy"), None),
            P(("gx", "gy"), None),
            P(("gx", "gy"), None),
            P(("gx", "gy"), None),
        ),
        out_specs=(
            P(("gx", "gy"), None, None, None, None),
            P(("gx", "gy"), None, None, None, None),
            P(),
        ),
        check_vma=False,
    )
```

```python
import math

import jax
import jax.numpy as jnp
from jax import lax
from jax.experimental import pallas as pl
from jax.experimental.pallas import tpu as pltpu
from jax.sharding import PartitionSpec as P

MESH = pl.DeviceIdType.MESH
FACES = ((-1, 0), (1, 0), (0, -1), (0, 1))
EDGES = ((-1, -1), (-1, 1), (1, -1), (1, 1))
TOWARD = FACES + EDGES
CH = 128
BRICKS = 4
OWN = 1792
HALF = OWN // 2
PART1 = HALF // 4
PART2 = PART1 // 4
ZROWS = 16
F32 = jnp.float32
BF16 = jnp.bfloat16


def step_kernel(
    n_gx, n_gy, scale,
    feat, ograd, kern_hbm, vmask, nbr, fsend, esend,
    outv, igv, full,
    raw_a, raw_g, kern, act, maskf, xt_a, xt_g, yt_a, yt_g, ct_a, ct_g, ox, oy, oc, cols, gt, w2, acc,
    part, rc, red, r1, red1, r2, red2, rz, zsum, gz,
    in_s, halo_s, halo_r, c_s, c_r, a_s, a_r, b_s, b_r, z_s, z_r,
    gc_s, gc_r, ga_s, ga_r, gb_s, gb_r, gz_s, gz_r,
):
    raw, xt, yt, ct = (raw_a, raw_g), (xt_a, xt_g), (yt_a, yt_g), (ct_a, ct_g)
    loads = [
        pltpu.make_async_copy(feat, raw_a, in_s.at[0]),
        pltpu.make_async_copy(ograd, raw_g, in_s.at[1]),
        pltpu.make_async_copy(kern_hbm, kern, in_s.at[2]),
    ]
    for load in loads:
        load.start()

    a = lax.axis_index("gx")
    b = lax.axis_index("gy")
    z = a // 2
    y = b // 4
    x = (a % 2) * 2 + (b // 2) % 2
    core = b % 2

    def device(x_, y_, z_, c_):
        return (z_ * 2 + x_ // 2, y_ * 4 + (x_ % 2) * 2 + c_)

    first_at = (x, y)
    second_at = (y, x)

    def peer_x(k):
        return device((x + k) % 4, y, z, core)

    def peer_y(k):
        return device(x, (y + k) % 4, z, core)

    def exists(d):
        return (a + d[0] >= 0) & (a + d[0] < n_gx) & (b + d[1] >= 0) & (b + d[1] < n_gy)

    partner = device(x, y, z, 1 - core)
    near = ([peer_x(k) for k in range(1, 4)], [peer_y(k) for k in range(1, 4)])
    peersz = [device(x, y, (z + k) % 8, core) for k in range(1, 8)]

    barrier = pltpu.get_barrier_semaphore()
    for peer in peersz + near[0] + near[1] + [partner]:
        pl.semaphore_signal(barrier, inc=1, device_id=peer, device_id_type=MESH)
    expected = 14
    for d in TOWARD:
        there = exists(d)
        expected = expected + there.astype(jnp.int32)

        @pl.when(there)
        def _():
            pl.semaphore_signal(barrier, inc=1, device_id=(a + d[0], b + d[1]), device_id_type=MESH)

    for s in range(BRICKS):
        for g in range(4):
            row = vmask[s : s + 1, g * 128 : (g + 1) * 128].astype(F32)
            tile = jnp.broadcast_to(row, (128, 128)).T
            maskf[s, 2 * g : 2 * g + 2] = tile.reshape(2, 8, 8, CH)

    def far(step):
        return 7 if step > 0 else 0

    def gather_rims(w):
        for i, d in enumerate(TOWARD):
            for j in range(2 if i < 4 else 1):
                entry = fsend[j, i] if i < 4 else esend[j, i - 4]
                spot = jnp.minimum(entry, BRICKS - 1)
                live = (entry < BRICKS).astype(F32)
                if i < 2:
                    keep = maskf[spot, far(d[0])] * live
                    ox[i, w, j] = (raw[w][spot, far(d[0])].astype(F32) * keep).astype(BF16)
                elif i < 4:
                    keep = maskf[spot, :, far(d[1])] * live
                    oy[i - 2, w, j] = (raw[w][spot, :, far(d[1])].astype(F32) * keep).astype(BF16)
                else:
                    keep = maskf[spot, far(d[0]), far(d[1])] * live
                    oc[i - 4, w, j] = (raw[w][spot, far(d[0]), far(d[1])].astype(F32) * keep).astype(BF16)

    def landing(d, w):
        e = (-d[0], -d[1])
        k = TOWARD.index(e)
        if k < 2:
            return xt[w].at[k, pl.ds(4 + 2 * k, 2)]
        if k < 4:
            return yt[w].at[k - 2, pl.ds(4 + 2 * k, 2)]
        return ct[w].at[k - 4, pl.ds(12 + k - 4, 1)]

    def halo_copy(i, w):
        d = TOWARD[i]
        source = ox.at[i, w] if i < 2 else (oy.at[i - 2, w] if i < 4 else oc.at[i - 4, w])
        return pltpu.make_async_remote_copy(
            src_ref=source, dst_ref=landing(d, w), send_sem=halo_s.at[w, i], recv_sem=halo_r.at[w, i],
            device_id=(a + d[0], b + d[1]), device_id_type=MESH,
        )

    def send_rims(w):
        for i, d in enumerate(TOWARD):
            @pl.when(exists(d))
            def _():
                halo_copy(i, w).start()

    def await_rims(w):
        for i, d in enumerate(TOWARD):
            @pl.when(exists((-d[0], -d[1])))
            def _():
                halo_copy(i, w).wait_recv()

        for corner, e in enumerate(EDGES):
            side_x = (e[0] + 1) // 2
            side_y = (e[1] + 1) // 2
            for j in range(2):
                ct[w][corner, 4 + 2 * side_x + j] = xt[w][side_x, 4 + 2 * side_x + j, far(-e[1])]
                ct[w][corner, 8 + 2 * side_y + j] = yt[w][side_y, 8 + 2 * side_y + j, far(-e[0])]

    loads[0].wait()
    gather_rims(0)
    pl.semaphore_wait(barrier, expected)
    send_rims(0)
    loads[1].wait()
    gather_rims(1)

    for d in TOWARD:
        @pl.when(jnp.logical_not(exists((-d[0], -d[1]))))
        def _():
            for w in range(2):
                spot = landing(d, w)
                spot[...] = jnp.zeros(spot.shape, BF16)

    level = lax.broadcasted_iota(jnp.int32, (1, 8, CH), 1)

    def place(k):
        return slice(k * CH, (k + 1) * CH)

    @pl.loop(0, BRICKS)
    def _(s):
        @pl.loop(0, 8)
        def _(i):
            m = maskf[s, i]
            for w in range(2):
                mid = raw[w][s, i].astype(F32) * m
                act[w, s, i] = mid.astype(BF16)
                down = jnp.where(level == 0, 0.0, pltpu.roll(mid, 1, 1))
                up = jnp.where(level == 7, 0.0, pltpu.roll(mid, 7, 1))
                for k, value in enumerate((down, mid, up)):
                    inner = value[1:7].reshape(48, CH).astype(BF16)
                    cols[w, s, i + 1, 0, 16:64, place(k)] = inner
                    cols[w, s, i + 1, 1, :, place(k)] = value.reshape(64, CH).astype(BF16)
                    cols[w, s, i + 1, 2, 0:48, place(k)] = inner

    for w in range(2):
        for side in range(2):
            xt[w][side, 16] = jnp.zeros((8, 8, CH), BF16)
            yt[w][side, 16] = jnp.zeros((8, 8, CH), BF16)
            for s in range(BRICKS):
                xt[w][side, s] = act[w, s, 7 - 7 * side]
                yt[w][side, s] = act[w, s, :, 7 - 7 * side]
        for corner, e in enumerate(EDGES):
            ct[w][corner, 16] = jnp.zeros((8, CH), BF16)
            for s in range(BRICKS):
                ct[w][corner, s] = act[w, s, far(-e[0]), far(-e[1])]

    @pl.loop(0, BRICKS)
    def _(s):
        for g in range(4):
            rows_ = act[1, s, 2 * g : 2 * g + 2].astype(F32).reshape(128, CH)
            gt[s, :, g * 128 : (g + 1) * 128] = rows_.T.astype(BF16)

    part[27 * CH : 28 * CH] = jnp.zeros((CH, CH), F32)
    red2[2 * PART2 : 8 * ZROWS] = jnp.zeros((8 * ZROWS - 2 * PART2, CH), F32)

    await_rims(0)
    send_rims(1)

    def shifted(below, here, above):
        down = jnp.where(level == 0, pltpu.roll(below, 1, 1), pltpu.roll(here, 1, 1))
        up = jnp.where(level == 7, pltpu.roll(above, 7, 1), pltpu.roll(here, 7, 1))
        return down, here, up

    def outer_columns(w):
        @pl.loop(0, BRICKS)
        def _(s):
            for side in range(2):
                column = 18 * side
                mids = [xt[w][side, nbr[s, column + 3 + k]].astype(F32) for k in range(3)]
                lows = [ct[w][2 * side, nbr[s, column + k]].astype(F32).reshape(1, 8, CH) for k in range(3)]
                highs = [ct[w][2 * side + 1, nbr[s, column + 6 + k]].astype(F32).reshape(1, 8, CH) for k in range(3)]
                whole = [jnp.concatenate([lows[k], mids[k], highs[k]], axis=0) for k in range(3)]
                for k, value in enumerate(shifted(*whole)):
                    for q in range(3):
                        cols[w, s, 9 * side, q, :, place(k)] = value[q : q + 8].reshape(64, CH).astype(BF16)

            low_at = [nbr[s, 9 + k] for k in range(3)]
            high_at = [nbr[s, 15 + k] for k in range(3)]

            @pl.loop(0, 8)
            def _(i):
                first = act[w, s, i, 0].astype(F32).reshape(1, 8, CH)
                last = act[w, s, i, 7].astype(F32).reshape(1, 8, CH)
                zero = jnp.zeros((1, 8, CH), F32)
                lows = [yt[w][0, low_at[k], i].astype(F32).reshape(1, 8, CH) for k in range(3)]
                highs = [yt[w][1, high_at[k], i].astype(F32).reshape(1, 8, CH) for k in range(3)]
                inner = [(zero, zero), (first, last), (zero, zero)]
                whole = [jnp.concatenate([lows[k], inner[k][0], inner[k][1], highs[k]], axis=0) for k in range(3)]
                for k, value in enumerate(shifted(*whole)):
                    cols[w, s, i + 1, 0, 0:16, place(k)] = value[0:2].reshape(16, CH).astype(BF16)
                    cols[w, s, i + 1, 2, 48:64, place(k)] = value[2:4].reshape(16, CH).astype(BF16)

    outer_columns(0)

    def columns(w, s, first, k):
        return cols[w, s, pl.ds(first, 8), k].reshape(512, 3 * CH)

    def weight_unit(i):
        u = i + (1 - core) * (8 - 2 * i)
        n = u // 3
        k = u % 3
        total = jnp.dot(gt[0], columns(0, 0, n, k), preferred_element_type=F32)
        for s in range(1, BRICKS):
            total = total + jnp.dot(gt[s], columns(0, s, n, k), preferred_element_type=F32)
        for q in range(3):
            part[pl.ds(pl.multiple_of((3 * u + q) * CH, CH), CH)] = total[:, place(q)].T

    def convolve(s):
        @pl.loop(0, 2)
        def _(w):
            for first in range(3):
                value = jnp.concatenate([columns(w, s, first, k) for k in range(3)], axis=1)
                weight = w2[w, 3 * first : 3 * first + 3].reshape(9 * CH, CH)
                term = jnp.dot(value, weight, preferred_element_type=F32)
                if first == 0:
                    acc[...] = term
                elif first == 1:
                    acc[...] += term
                else:
                    term = (acc[...] + term) * maskf[s].reshape(512, CH)
                    result = term.reshape(8, 8, 8, CH).astype(BF16)

                    @pl.when(w == 0)
                    def _():
                        outv[s] = result

                    @pl.when(w == 1)
                    def _():
                        igv[s] = result

    def remote(source, target, sems, semr, k, peer):
        return pltpu.make_async_remote_copy(
            src_ref=source, dst_ref=target, send_sem=sems.at[k], recv_sem=semr.at[k],
            device_id=peer, device_id_type=MESH,
        )

    def start(copies):
        for copy in copies:
            copy.start()
        return copies

    sent = []

    def finish(copies):
        for copy in copies:
            copy.wait_recv()
            sent.append(copy)

    def rows(start, size, unit):
        return pl.ds(pl.multiple_of(start, unit), size)

    mine = core * OWN
    other = (1 - core) * OWN
    order = (2, 1, 3, 0)

    def chunk(h, p, base=0):
        return rows(base + h * HALF + p % 4 * PART1, PART1, PART1)

    @pl.loop(0, 5)
    def _(i):
        weight_unit(i)

    steps = [(k, h) for k in order for h in range(2)]
    pair = start([
        remote(part.at[chunk(h, first_at[h] + k, other)], rc.at[chunk(h, first_at[h] + k)], c_s, c_r, j, partner)
        for j, (k, h) in enumerate(steps)
    ])

    @pl.loop(5, 9)
    def _(i):
        weight_unit(i)

    first = []
    for j, (k, h) in enumerate(steps):
        finish([pair[j]])
        base = h * HALF + (first_at[h] + k) % 4 * PART1

        at = rows(base, PART1, PART1)
        red[at] = part[rows(mine + base, PART1, PART1)] + rc[at]

        if k:
            first += start([remote(red.at[chunk(h, first_at[h] + k)], r1.at[h, k - 1], a_s.at[h], a_r.at[h], k - 1, near[h][k - 1])])

    loads[2].wait()

    @pl.loop(0, 9)
    def _(n):
        for k in range(3):
            w2[0, n, k * CH : (k + 1) * CH] = kern[3 * n + k]
            w2[1, n, k * CH : (k + 1) * CH] = kern[26 - 3 * n - k].astype(F32).T.astype(BF16)

    await_rims(1)
    outer_columns(1)
    convolve(0)
    finish(first)

    second = []
    for h in range(2):
        own = red[rows(h * HALF + first_at[h] * PART1, PART1, PART1)]
        red1[h] = own + r1[h, 0] + r1[h, 1] + r1[h, 2]

        second += start([
            remote(
                red1.at[h, rows((second_at[h] + k) % 4 * PART2, PART2, PART2)], r2.at[h, k - 1],
                b_s.at[h], b_r.at[h], k - 1, near[1 - h][k - 1],
            )
            for k in range(1, 4)
        ])
    convolve(1)
    finish(second)
    for h in range(2):
        own = red1[h, rows(second_at[h] * PART2, PART2, PART2)]
        red2[h * PART2 : (h + 1) * PART2] = own + r2[h, 0] + r2[h, 1] + r2[h, 2]
    third = start([
        remote(red2.at[rows((z + k) % 8 * ZROWS, ZROWS, ZROWS)], rz.at[k - 1], z_s, z_r, k - 1, peersz[k - 1])
        for k in range(1, 8)
    ])
    convolve(2)
    finish(third)
    level_rows = rows(z * ZROWS, ZROWS, ZROWS)
    total = red2[level_rows]
    for k in range(7):
        total = total + rz[k]
    zsum[...] = total / scale
    gz[level_rows] = zsum[...]
    fourth = start([remote(zsum, gz.at[level_rows], gz_s, gz_r, k - 1, peersz[k - 1]) for k in range(1, 8)])
    convolve(3)
    finish(fourth)
    spread = []
    for h in range(2):
        spot2 = rows(mine + h * HALF + first_at[h] * PART1 + second_at[h] * PART2, PART2, PART2)
        full[spot2] = gz[h * PART2 : (h + 1) * PART2]
        spread += start([
            remote(full.at[spot2], full.at[spot2], gb_s.at[h], gb_r.at[h], k - 1, near[1 - h][k - 1])
            for k in range(1, 4)
        ])
    finish(spread)

    def hand(h, k):
        at = chunk(h, first_at[h] + 4 - k, mine)
        return remote(full.at[at], full.at[at], gc_s.at[h], gc_r.at[h], k, partner)

    last = {}
    for k in (2, 1, 3):
        for h in range(2):
            spot1 = chunk(h, first_at[h], mine)
            last[h, k] = remote(full.at[spot1], full.at[spot1], ga_s.at[h], ga_r.at[h], k - 1, near[h][k - 1])
            last[h, k].start()
    hands = start([hand(h, 0) for h in range(2)])
    for k in (1, 3, 2):
        for h in range(2):
            finish([last[h, k]])
            hands += start([hand(h, k)])
    finish(hands)
    for copy in sent:
        copy.wait_send()
    for w in range(2):
        for i, d in enumerate(TOWARD):
            @pl.when(exists(d))
            def _():
                halo_copy(i, w).wait_send()


def store_kernel(outv, igv, full, out_hbm, ig_hbm, wg_hbm, sem):
    copies = [
        pltpu.make_async_copy(full.at[0 : 27 * CH], wg_hbm, sem.at[0]),
        pltpu.make_async_copy(outv, out_hbm, sem.at[1]),
        pltpu.make_async_copy(igv, ig_hbm, sem.at[2]),
    ]
    for copy in copies:
        copy.start()
    for copy in copies:
        copy.wait()


def solution(mesh):
    n_gx = mesh.shape["gx"]
    n_gy = mesh.shape["gy"]

    def local(features, out_grad, kernel, voxel_mask, neighbours, face_sends, edge_sends):
        scale = math.sqrt(n_gx * n_gy * BRICKS * 512)
        vmem = pl.BlockSpec(memory_space=pltpu.VMEM)
        smem = pl.BlockSpec(memory_space=pltpu.SMEM)
        anywhere = pl.BlockSpec(memory_space=pl.ANY)
        dma = pltpu.SemaphoreType.DMA
        brick = (8, 8, 8, CH)
        held = pl.pallas_call(
            lambda *refs: step_kernel(n_gx, n_gy, scale, *refs),
            out_shape=(
                pltpu.VMEM((BRICKS,) + brick, BF16),
                pltpu.VMEM((BRICKS,) + brick, BF16),
                pltpu.VMEM((2 * OWN, CH), F32),
            ),
            in_specs=[anywhere, anywhere, anywhere, vmem, smem, smem, smem],
            out_specs=(vmem, vmem, vmem),
            scratch_shapes=[
                pltpu.VMEM((BRICKS,) + brick, BF16),
                pltpu.VMEM((BRICKS,) + brick, BF16),
                pltpu.VMEM((27, CH, CH), BF16),
                pltpu.VMEM((2, BRICKS) + brick, BF16),
                pltpu.VMEM((BRICKS,) + brick, F32),
                pltpu.VMEM((2, 17, 8, 8, CH), BF16),
                pltpu.VMEM((2, 17, 8, 8, CH), BF16),
                pltpu.VMEM((2, 17, 8, 8, CH), BF16),
                pltpu.VMEM((2, 17, 8, 8, CH), BF16),
                pltpu.VMEM((4, 17, 8, CH), BF16),
                pltpu.VMEM((4, 17, 8, CH), BF16),
                pltpu.VMEM((2, 2, 2, 8, 8, CH), BF16),
                pltpu.VMEM((2, 2, 2, 8, 8, CH), BF16),
                pltpu.VMEM((4, 2, 1, 8, CH), BF16),
                pltpu.VMEM((2, BRICKS, 10, 3, 64, 3 * CH), BF16),
                pltpu.VMEM((BRICKS, CH, 512), BF16),
                pltpu.VMEM((2, 9, 3 * CH, CH), BF16),
                pltpu.VMEM((512, CH), F32),
                pltpu.VMEM((2 * OWN, CH), F32),
                pltpu.VMEM((OWN, CH), F32),
                pltpu.VMEM((OWN, CH), F32),
                pltpu.VMEM((2, 3, PART1, CH), F32),
                pltpu.VMEM((2, PART1, CH), F32),
                pltpu.VMEM((2, 3, PART2, CH), F32),
                pltpu.VMEM((8 * ZROWS, CH), F32),
                pltpu.VMEM((7, ZROWS, CH), F32),
                pltpu.VMEM((ZROWS, CH), F32),
                pltpu.VMEM((8 * ZROWS, CH), F32),
                dma((3,)), dma((2, 8)), dma((2, 8)),
                dma((8,)), dma((8,)), dma((2, 3)), dma((2, 3)), dma((2, 3)), dma((2, 3)), dma((7,)), dma((7,)),
                dma((2, 4)), dma((2, 4)), dma((2, 3)), dma((2, 3)), dma((2, 3)), dma((2, 3)), dma((7,)), dma((7,)),
            ],
            compiler_params=pltpu.CompilerParams(collective_id=0, has_side_effects=True),
            name="step",
        )(features, out_grad, kernel, voxel_mask, neighbours, face_sends.T, edge_sends.T)
        output, input_grad, weight = pl.pallas_call(
            store_kernel,
            out_shape=(
                jax.ShapeDtypeStruct((BRICKS,) + brick, BF16),
                jax.ShapeDtypeStruct((BRICKS,) + brick, BF16),
                jax.ShapeDtypeStruct((27 * CH, CH), F32),
            ),
            in_specs=[vmem, vmem, vmem],
            out_specs=(anywhere, anywhere, anywhere),
            scratch_shapes=[dma((3,))],
            name="store",
        )(*(pltpu.with_memory_space_constraint(h, pltpu.VMEM) for h in held))
        return output, input_grad, weight.reshape(27, CH, CH)

    return jax.shard_map(
        local,
        mesh=mesh,
        in_specs=(
            P(("gx", "gy"), None, None, None, None),
            P(("gx", "gy"), None, None, None, None),
            P(),
            P(("gx", "gy"), None),
            P(("gx", "gy"), None),
            P(("gx", "gy"), None),
            P(("gx", "gy"), None),
        ),
        out_specs=(
            P(("gx", "gy"), None, None, None, None),
            P(("gx", "gy"), None, None, None, None),
            P(),
        ),
        check_vma=False,
    )
```
